768 devices in a mesh: prow: 64 (over x, y, core), pcol: 12 (over z).
Axes of the slice: x: 4, y: 8, z: 12, core: 2. Of those that a mesh axis runs over, the one named last changes fastest.
Arguments:
- matrix: bfloat16 [131072, 6144], P('prow', 'pcol')
- pivots: int32 [512], replicated, may hold values from 512 to 131071, as said below
- unit_inverse: bfloat16 [512, 512], replicated, as said below
Outputs:
- factored: bfloat16 [131072, 6144], P('prow', 'pcol')
The draws below stay inside these ranges and needn't reach their ends.
Inputs may be any that keep to these rules, and one draw needn't show every extreme that they name: pivots are distinct rows, none among the first 512. unit_inverse is unit lower triangular.
All inputs are finite; a program needn't handle non-finite values.
Results may differ from the reference program's by a relative error of at most 0.0041.
Values may be sent and summed in bfloat16 or wider, within the bound.
A program may use at most 32 MiB of HBM per device.

```python
import jax
import jax.numpy as jnp
from jax import lax

NB = 512
N = 6144
ROWS_DEV = 2048
M = 131072
N_PROW = 64


def draw_matrix(key, part):
    values = jax.random.normal(key, (M, N), jnp.float32)
    column_scale = jnp.where(jnp.arange(N) < NB, NB ** (-0.5), 1.0)
    return (values * column_scale[None, :]).astype(jnp.bfloat16)


def draw_unit_inverse(key, part):
    values = jax.random.normal(key, (NB, NB), jnp.float32)
    lower = jnp.tril(values * NB ** (-0.5), -1)
    return (lower + jnp.eye(NB, dtype=jnp.float32)).astype(jnp.bfloat16)


def draw_pivots(key, part):
    key_weight = jax.random.fold_in(key, 11)
    key_score = jax.random.fold_in(key, 12)
    key_forced = jax.random.fold_in(key, 13)
    row_ids = jnp.arange(M, dtype=jnp.int32)
    weights = jax.random.randint(key_weight, (M // ROWS_DEV,), 1, 4)
    row_weight = weights[row_ids // ROWS_DEV]
    scores = jax.random.randint(key_score, (M,), 0, 1024) * row_weight
    owners = jnp.array([1, N_PROW // 2, N_PROW - 1], dtype=jnp.int32)
    offsets = jax.random.randint(key_forced, (3,), 0, ROWS_DEV)
    forced_rows = owners * ROWS_DEV + offsets
    forced = jnp.any(row_ids[:, None] == forced_rows[None, :], axis=1)
    scores = jnp.where(forced, 4096, scores)
    keyed = jnp.where(row_ids >= NB, scores * M + row_ids, -1 - row_ids)
    chosen = lax.top_k(keyed, NB)[1]
    return chosen.astype(jnp.int32)


def setup_inputs(seed: int = 0) -> dict:
    key_list = jax.random.split(jax.random.key(seed), 4)
    return {
        "matrix": draw_matrix(jax.random.fold_in(key_list[3], 71), 0),
        "pivots": draw_pivots(jax.random.fold_in(key_list[3], 71), 0),
        "unit_inverse": draw_unit_inverse(jax.random.fold_in(key_list[3], 71), 0),
    }


def reference(matrix, pivots, unit_inverse):
    count = unit_inverse.shape[0]
    total_rows = matrix.shape[0]
    leading = jnp.arange(count, dtype=jnp.int32)
    swapped = matrix.at[leading].set(matrix[pivots]).at[pivots].set(matrix[:count])
    upper = jnp.dot(unit_inverse, swapped[:count], preferred_element_type=jnp.float32).astype(jnp.bfloat16)
    blocks = swapped.reshape(N_PROW, total_rows // N_PROW, swapped.shape[1])
    factors = matrix[:, :count].reshape(N_PROW, total_rows // N_PROW, count)

    def update_block(pair):
        block, factor = pair
        return (block.astype(jnp.float32) - jnp.dot(factor, upper, preferred_element_type=jnp.float32)).astype(jnp.bfloat16)

    updated = lax.map(update_block, (blocks, factors)).reshape(total_rows, swapped.shape[1])
    updated = updated.at[:count].set(upper)
    return updated.at[:, :count].set(matrix[:, :count])
```

```python
import functools

import jax
import jax.numpy as jnp
from jax import lax
from jax.experimental import pallas as pl
from jax.experimental.pallas import tpu as pltpu
from jax.sharding import PartitionSpec as P

MESH = pl.DeviceIdType.MESH
F32 = jnp.float32
BF16 = jnp.bfloat16

R = 32
N_PLUS, N_BOTH, REACH = 36, 18, 4
NX, NY, NZ = 4, 8, 12
BLK = 256

R1, R2, R3, G1, G2, G3, D0A, D0B, D0C, D2, D3, NSEM = 0, 1, 4, 11, 18, 21, 22, 23, 26, 33, 36, 37


def kernel(mat, piv, inv, out, pan, mv, swp, acc, pcol_s, pk, rc, s1, rx, s2, ry, s3, g1, g, dd, d1, d, up,
           ss, rs, ps, pr, bs, br, ls, os):
    z = lax.axis_index("pcol")
    row = lax.axis_index("prow")
    rows_dev, cols = mat.shape
    width = piv.shape[1]
    half = cols // 2
    core = lax.rem(row, 2)
    y = lax.rem(row // 2, NY)
    x = row // (2 * NY)
    mate = row + 1 - 2 * core
    n_chunk = rows_dev // R
    n_minus = n_chunk - N_PLUS - N_BOTH
    xrows, yrows = width // NX, width // NX // NY

    above, below = lax.rem(z + 1, NZ), lax.rem(z + NZ - 1, NZ)
    src_z = jnp.where(core == 1, below, above)
    dst_z = jnp.where(core == 1, above, below)
    hop = jnp.where(core == 1, z, lax.rem(NZ - z, NZ))
    single = jnp.where(core == 1, 2 * N_PLUS, 2 * n_minus)
    total = single + 2 * N_BOTH
    reach = jnp.where(core == 1, REACH, NZ - 1 - REACH)
    n_in = jnp.where(hop <= reach, total, single)
    n_out = jnp.where(hop == NZ - 1, 0, jnp.where(hop < reach, total, single))

    def item(i):
        k = i - single
        up_p = jnp.where(i < N_PLUS, 1, jnp.where(i < 2 * N_PLUS, 0, 1 - lax.rem(k + 2 * n_chunk, 2)))
        up_c = jnp.where(i < N_PLUS, i, jnp.where(i < 2 * N_PLUS, i - N_PLUS, N_PLUS + (k + 2 * n_chunk) // 2 - n_chunk))
        dn_p = lax.rem(i, 2)
        dn_c = jnp.where(i < 2 * n_minus, N_PLUS + N_BOTH + i // 2, N_PLUS + (k + 2 * n_chunk) // 2 - n_chunk)
        return jnp.where(core == 1, up_p, dn_p), jnp.where(core == 1, up_c, dn_c)

    def chunk(c):
        return pl.ds(pl.multiple_of(c * R, R), R)

    def ring(i, own):
        p, c = item(i)
        return pltpu.make_async_remote_copy(
            mat.at[chunk(c)] if own else pan.at[p, chunk(c)], pan.at[p, chunk(c)], ss.at[i], rs.at[i],
            device_id={"pcol": dst_z}, device_id_type=MESH)

    def hand_over(c, p):
        return pltpu.make_async_remote_copy(
            pan.at[p, chunk(c)], pan.at[p, chunk(c)], ps.at[c], pr.at[c], device_id={"prow": mate}, device_id_type=MESH)

    def bulk(c0, n, p):
        part = pl.ds(c0 * R, n * R)
        return pltpu.make_async_remote_copy(
            mat.at[part], pan.at[p, part], ps.at[0], pr.at[0], device_id={"prow": mate}, device_id_type=MESH)

    def mine(c):
        return jnp.where(core == 1, (c < N_PLUS) | ((c < N_PLUS + N_BOTH) & (z <= REACH)),
                         (c >= N_PLUS + N_BOTH) | ((c >= N_PLUS) & (z > REACH)))

    def prow_of(px, py):
        return (px * NY + py) * 2 + core

    def xpeer(k):
        return lax.rem(x + k, NX)

    def ypeer(k):
        return lax.rem(y + k, NY)

    pltpu.make_async_copy(mat, mv, ls.at[0]).start()
    bar = pltpu.get_barrier_semaphore()

    def greet(**where):
        pl.semaphore_signal(bar, inc=1, device_id=where, device_id_type=MESH)

    greet(prow=mate)

    @pl.when(z > 0)
    def _():
        greet(pcol=src_z)
        for k in range(1, NX):
            greet(prow=prow_of(xpeer(k), y))
        for k in range(1, NY):
            greet(prow=prow_of(x, ypeer(k)))

    @pl.when(z == 0)
    def _():
        pl.semaphore_wait(bar, 2)

        @pl.when(core == 0)
        def _():
            bulk(0, N_PLUS + N_BOTH, 0).start()

        @pl.when(core == 1)
        def _():
            bulk(N_PLUS, n_chunk - N_PLUS, 1).start()

        @pl.loop(0, total)
        def _(i):
            @pl.when((core == 1) & (i == N_PLUS))
            def _():
                bulk(0, N_PLUS + N_BOTH, 0).wait_recv()

            @pl.when((core == 0) & (i == 0))
            def _():
                bulk(N_PLUS, n_chunk - N_PLUS, 1).wait_recv()

            p, _ = item(i)

            @pl.when(p == core)
            def _():
                ring(i, True).start()

            @pl.when(p != core)
            def _():
                ring(i, False).start()

        pltpu.make_async_copy(mat, mv, ls.at[0]).wait()
        keep = pltpu.make_async_copy(mv, out, os.at[0])
        keep.start()
        keep.wait()

        @pl.when(core == 0)
        def _():
            bulk(0, N_PLUS + N_BOTH, 0).wait_send()

        @pl.when(core == 1)
        def _():
            bulk(N_PLUS, n_chunk - N_PLUS, 1).wait_send()

        @pl.loop(0, total)
        def _(i):
            ring(i, True).wait_send()

    @pl.when(z > 0)
    def _():
        base = row * rows_dev
        pltpu.make_async_copy(mat, mv, ls.at[0]).wait()

        pcol_s[...] = jnp.transpose(jnp.broadcast_to(piv[...], (128, width)))
        acc[...] = jnp.zeros_like(acc)

        @pl.loop(0, rows_dev // BLK)
        def _(b):
            lane = lax.broadcasted_iota(jnp.int32, (width, 128), 1) + (base + b * BLK)
            hit = [jnp.where(pcol_s[...] == lane + 128 * j, 1.0, 0.0).astype(BF16) for j in range(BLK // 128)]
            acc[...] += jnp.dot(jnp.concatenate(hit, axis=1), mv[pl.ds(pl.multiple_of(b * BLK, BLK), BLK), :],
                                preferred_element_type=F32)

        for h in range(2):
            pk[h] = acc[:, h * half:(h + 1) * half].astype(BF16)

        pl.semaphore_wait(bar, NX + NY - 1 + jnp.where(hop < NZ - 1, 1, 0))

        def send(src, dst, number, prow, recv=None):
            return pltpu.make_async_remote_copy(
                src, dst, bs.at[number], br.at[number if recv is None else recv],
                device_id={"prow": prow}, device_id_type=MESH)

        def xrow(k):
            return pl.ds(pl.multiple_of(k * xrows, xrows), xrows)

        def yrow(k):
            return pl.ds(pl.multiple_of(k * yrows, yrows), yrows)

        c_r1 = send(pk.at[1 - core], rc, R1, mate)
        c_r2 = [send(s1.at[xrow(xpeer(k))], rx.at[k - 1], R2 + k - 1, prow_of(xpeer(k), y)) for k in range(1, NX)]
        c_r3 = [send(s2.at[yrow(ypeer(k))], ry.at[k - 1], R3 + k - 1, prow_of(x, ypeer(k))) for k in range(1, NY)]
        c_g1 = [send(s3, g1.at[yrow(y)], G1 + k - 1, prow_of(x, ypeer(k))) for k in range(1, NY)]
        c_g2 = [send(g1, g.at[core, xrow(x)], G2 + k - 1, prow_of(xpeer(k), y)) for k in range(1, NX)]
        c_g3 = send(g.at[core], g.at[core], G3, mate)
        c_d0a = send(mv.at[pl.ds(0, width), pl.ds(half, half)], dd, D0A, mate)
        c_d0b = [send(mv.at[pl.ds(k * xrows, xrows), pl.ds(0, half)], d1, D0B + k - 1, prow_of(k, y), D0B) for k in range(1, NX)]
        c_d0b1 = [send(dd.at[pl.ds(k * xrows, xrows)], d1, D0B + k - 1, prow_of(k, y), D0B) for k in range(1, NX)]
        c_d0c = [send(d1, d1, D0C + k - 1, prow_of(x, k), D0C) for k in range(1, NY)]
        c_d2 = [send(d1, d.at[core, xrow(x)], D2 + k - 1, prow_of(xpeer(k), y)) for k in range(1, NX)]
        c_d3 = send(d.at[core], d.at[core], D3, mate)
        l_d1a = pltpu.make_async_copy(mv.at[pl.ds(0, xrows), pl.ds(0, half)], d1, ls.at[1])
        l_d1b = pltpu.make_async_copy(dd.at[pl.ds(0, xrows)], d1, ls.at[1])
        l_d = pltpu.make_async_copy(d1, d.at[core, xrow(x)], ls.at[2])
        l_g = pltpu.make_async_copy(g1, g.at[core, xrow(x)], ls.at[3])
        first = (x == 0) & (y == 0)

        c_r1.start()

        @pl.when(first & (core == 0))
        def _():
            c_d0a.start()
            l_d1a.start()
            for cp in c_d0b:
                cp.start()

        def step1():
            @pl.when(first & (core == 1))
            def _():
                c_d0a.wait_recv()
                l_d1b.start()
                for cp in c_d0b1:
                    cp.start()

        def step2():
            c_r1.wait_recv()
            s1[...] = (pk[core].astype(F32) + rc[...].astype(F32)).astype(BF16)
            for cp in c_r2:
                cp.start()

        def step3():
            @pl.when(y == 0)
            def _():
                @pl.when(x == 0)
                def _():
                    l_d1a.wait()

                @pl.when(x > 0)
                def _():
                    c_d0b[0].wait_recv()

                for cp in c_d0c:
                    cp.start()

        def step4():
            for cp in c_r2:
                cp.wait_recv()
            got = s1[xrow(x), :].astype(F32)
            for k in range(NX - 1):
                got += rx[k].astype(F32)
            s2[...] = got.astype(BF16)
            for cp in c_r3:
                cp.start()

        def step5():
            @pl.when(y > 0)
            def _():
                c_d0c[0].wait_recv()

            l_d.start()
            for cp in c_d2:
                cp.start()

        def step6():
            for cp in c_r3:
                cp.wait_recv()
            got = s2[yrow(y), :].astype(F32)
            for k in range(NY - 1):
                got += ry[k].astype(F32)
            s3[...] = got.astype(BF16)
            g1[yrow(y), :] = got.astype(BF16)
            for cp in c_g1:
                cp.start()

        def step7():
            l_d.wait()
            for cp in c_d2:
                cp.wait_recv()
            c_d3.start()

        def step8():
            for cp in c_g1:
                cp.wait_recv()
            l_g.start()
            for cp in c_g2:
                cp.start()

        def step9():
            c_d3.wait_recv()

        def step10():
            l_g.wait()
            for cp in c_g2:
                cp.wait_recv()
            c_g3.start()

        def step11():
            c_g3.wait_recv()
            for h in range(2):
                up[h] = jnp.dot(inv[...], g[h], preferred_element_type=F32).astype(BF16)

        def exchange(b):
            at = pl.ds(pl.multiple_of(b * BLK, BLK), BLK)
            hit = lax.broadcasted_iota(jnp.int32, (BLK, width), 0) + (base + b * BLK) == piv[...]
            one = jnp.where(hit, 1.0, 0.0)
            has = jnp.max(one, axis=1, keepdims=True) > 0.5
            one = one.astype(BF16)
            for h in range(2):
                here = slice(h * half, (h + 1) * half)
                moved = jnp.dot(one, d[h], preferred_element_type=F32)
                swp[at, here] = jnp.where(has, moved, mv[at, here].astype(F32)).astype(BF16)

        steps = ((21, step1), (23, step2), (31, step3), (37, step4), (52, step5), (54, step6), (67, step7), (69, step8),
                 (74, step9), (84, step10), (90, step11))
        lag = jnp.where(core == 1, 5 + 5 * z, 4 + 9 * (NZ - z))

        @pl.loop(0, jnp.maximum(lag + n_in, 92))
        def _(t):
            for when, step in steps:
                pl.when(t == when)(step)

            @pl.when((t >= 75) & (t < 83))
            def _():
                exchange(t - 75)

            i = t - lag

            @pl.when((i >= 0) & (i < n_in))
            def _():
                ring(i, False).wait_recv()

                @pl.when(i < n_out)
                def _():
                    ring(i, False).start()

                p, c = item(i)

                @pl.when(p != core)
                def _():
                    hand_over(c, p).start()

        def write(b):
            at = pl.ds(pl.multiple_of(b * BLK, BLK), BLK)
            return pltpu.make_async_copy(swp.at[at], out.at[at], os.at[b])

        @pl.loop(0, rows_dev // BLK)
        def _(k):
            b = jnp.where(z < NZ // 2, k, rows_dev // BLK - 1 - k)
            at = pl.ds(pl.multiple_of(b * BLK, BLK), BLK)

            @pl.loop(0, BLK // R)
            def _(j):
                c = b * (BLK // R) + j

                @pl.when(jnp.logical_not(mine(c)))
                def _():
                    hand_over(c, core).wait_recv()

            lead = (row == 0) & (b < width // BLK)

            @pl.when(lead)
            def _():
                for h in range(2):
                    swp[at, h * half:(h + 1) * half] = up[h, at, :]

            @pl.when(jnp.logical_not(lead))
            def _():
                left = pan[core, at, :]
                for h in range(2):
                    here = slice(h * half, (h + 1) * half)
                    swp[at, here] = (swp[at, here].astype(F32)
                                     - jnp.dot(left, up[h], preferred_element_type=F32)).astype(BF16)

            write(b).start()

        @pl.loop(0, n_chunk)
        def _(c):
            @pl.when(mine(c))
            def _():
                hand_over(c, 1 - core).wait_send()

        @pl.loop(0, n_out)
        def _(i):
            ring(i, False).wait_send()

        for cp in [c_r1, *c_r2, *c_r3, *c_g1, *c_g2, c_g3, *c_d2, c_d3]:
            cp.wait_send()

        @pl.when(first & (core == 0))
        def _():
            c_d0a.wait_send()

        @pl.when(first)
        def _():
            for cp in c_d0b1:
                cp.wait_send()

        @pl.when(y == 0)
        def _():
            for cp in c_d0c:
                cp.wait_send()

        @pl.loop(0, rows_dev // BLK)
        def _(b):
            write(b).wait()


def per_device(matrix, pivots, unit_inverse):
    rows, cols = matrix.shape
    width = unit_inverse.shape[0]
    half = cols // 2
    n_chunk = rows // R
    n_ring = 2 * N_BOTH + 2 * max(N_PLUS, n_chunk - N_PLUS - N_BOTH)
    xrows, yrows = width // NX, width // NX // NY
    dma = pltpu.SemaphoreType.DMA
    vm = pltpu.VMEM
    return pl.pallas_call(
        kernel,
        out_shape=jax.ShapeDtypeStruct(matrix.shape, matrix.dtype),
        in_specs=[
            pl.BlockSpec(memory_space=pl.ANY),
            pl.BlockSpec(memory_space=pltpu.VMEM),
            pl.BlockSpec(memory_space=pltpu.VMEM),
        ],
        out_specs=pl.BlockSpec(memory_space=pl.ANY),
        scratch_shapes=[
            vm((2, rows, cols), BF16),
            vm((rows, cols), BF16),
            vm((rows, cols), BF16),
            vm((width, cols), F32),
            vm((width, 128), jnp.int32),
            vm((2, width, half), BF16),
            vm((width, half), BF16),
            vm((width, half), BF16),
            vm((NX - 1, xrows, half), BF16),
            vm((xrows, half), BF16),
            vm((NY - 1, yrows, half), BF16),
            vm((yrows, half), BF16),
            vm((xrows, half), BF16),
            vm((2, width, half), BF16),
            vm((width, half), BF16),
            vm((xrows, half), BF16),
            vm((2, width, half), BF16),
            vm((2, width, half), BF16),
            dma((n_ring,)),
            dma((n_ring,)),
            dma((n_chunk,)),
            dma((n_chunk,)),
            dma((NSEM,)),
            dma((NSEM,)),
            dma((4,)),
            dma((rows // BLK,)),
        ],
        compiler_params=pltpu.CompilerParams(collective_id=0, has_side_effects=True),
        name="lu_step",
    )(matrix, pivots.reshape(1, width), unit_inverse)


def solution(mesh):
    return jax.shard_map(
        per_device,
        mesh=mesh,
        in_specs=(P("prow", "pcol"), P(), P()),
        out_specs=P("prow", "pcol"),
        check_vma=False,
    )
```

```python
import functools

import jax
import jax.numpy as jnp
from jax import lax
from jax.experimental import pallas as pl
from jax.experimental.pallas import tpu as pltpu
from jax.sharding import PartitionSpec as P

MESH = pl.DeviceIdType.MESH
F32 = jnp.float32
BF16 = jnp.bfloat16

R = 32
N_PLUS, N_BOTH, REACH = 38, 20, 4
NX, NY, NZ = 4, 8, 12
BLK = 256

R1, R2, R3, G1, G2, G3, D0A, D0B, D0C, D1, D2, D3, NSEM = 0, 1, 4, 11, 18, 21, 22, 23, 26, 33, 40, 43, 44


def kernel(mat, piv, inv, out, pan, mv, acc, pcol_s, pk, rc, s1, rx, s2, ry, s3, g1, g, dd, db, d0, d1, d, up,
           ss, rs, ps, pr, bs, br, ls):
    z = lax.axis_index("pcol")
    row = lax.axis_index("prow")
    rows_dev, cols = mat.shape
    width = piv.shape[1]
    half = cols // 2
    core = lax.rem(row, 2)
    y = lax.rem(row // 2, NY)
    x = row // (2 * NY)
    mate = row + 1 - 2 * core
    n_chunk = rows_dev // R
    n_minus = n_chunk - N_PLUS - N_BOTH
    xrows, yrows = width // NX, width // NX // NY

    above, below = lax.rem(z + 1, NZ), lax.rem(z + NZ - 1, NZ)
    src_z = jnp.where(core == 1, below, above)
    dst_z = jnp.where(core == 1, above, below)
    hop = jnp.where(core == 1, z, lax.rem(NZ - z, NZ))
    single = jnp.where(core == 1, 2 * N_PLUS, 2 * n_minus)
    total = single + 2 * N_BOTH
    reach = jnp.where(core == 1, REACH, NZ - 1 - REACH)
    n_in = jnp.where(hop <= reach, total, single)
    n_out = jnp.where(hop == NZ - 1, 0, jnp.where(hop < reach, total, single))

    def item(i):
        k = i - single
        up_p = jnp.where(i < N_PLUS, 1, jnp.where(i < 2 * N_PLUS, 0, 1 - lax.rem(k + 2 * n_chunk, 2)))
        up_c = jnp.where(i < N_PLUS, i, jnp.where(i < 2 * N_PLUS, i - N_PLUS, N_PLUS + (k + 2 * n_chunk) // 2 - n_chunk))
        dn_p = lax.rem(i, 2)
        dn_c = jnp.where(i < 2 * n_minus, N_PLUS + N_BOTH + i // 2, N_PLUS + (k + 2 * n_chunk) // 2 - n_chunk)
        return jnp.where(core == 1, up_p, dn_p), jnp.where(core == 1, up_c, dn_c)

    def chunk(c):
        return pl.ds(pl.multiple_of(c * R, R), R)

    def ring(i, own):
        p, c = item(i)
        return pltpu.make_async_remote_copy(
            mat.at[chunk(c)] if own else pan.at[p, chunk(c)], pan.at[p, chunk(c)], ss.at[i], rs.at[i],
            device_id={"pcol": dst_z}, device_id_type=MESH)

    def hand_over(c, p):
        return pltpu.make_async_remote_copy(
            pan.at[p, chunk(c)], pan.at[p, chunk(c)], ps.at[c], pr.at[c], device_id={"prow": mate}, device_id_type=MESH)

    def bulk(c0, n, p):
        part = pl.ds(c0 * R, n * R)
        return pltpu.make_async_remote_copy(
            mat.at[part], pan.at[p, part], ps.at[0], pr.at[0], device_id={"prow": mate}, device_id_type=MESH)

    def mine(c):
        return jnp.where(core == 1, (c < N_PLUS) | ((c < N_PLUS + N_BOTH) & (z <= REACH)),
                         (c >= N_PLUS + N_BOTH) | ((c >= N_PLUS) & (z > REACH)))

    def prow_of(px, py):
        return (px * NY + py) * 2 + core

    def xpeer(k):
        return lax.rem(x + k, NX)

    def ypeer(k):
        return lax.rem(y + k, NY)

    load = pltpu.make_async_copy(mat, mv, ls.at[0])
    keep = pltpu.make_async_copy(mat, out, ls.at[0])
    bar = pltpu.get_barrier_semaphore()

    def greet(**where):
        pl.semaphore_signal(bar, inc=1, device_id=where, device_id_type=MESH)

    @pl.when((z > 0) | (core == 1))
    def _():
        greet(prow=mate)

    @pl.when(z > 0)
    def _():
        load.start()
        greet(pcol=src_z)
        for k in range(1, NX):
            greet(prow=prow_of(xpeer(k), y))
        for k in range(1, NY):
            greet(prow=prow_of(x, ypeer(k)))

    @pl.when(z == 0)
    def _():
        pl.semaphore_wait(bar, 2 - core)
        keep.start()
        to_up = bulk(0, N_PLUS + N_BOTH, 0)
        to_down = bulk(N_PLUS, n_chunk - N_PLUS, 1)

        @pl.when(core == 0)
        def _():
            to_up.start()

        @pl.loop(0, total)
        def _(i):
            @pl.when((core == 1) & (i == N_PLUS))
            def _():
                to_up.wait_recv()
                to_down.start()

            @pl.when((core == 0) & (i == 0))
            def _():
                to_down.wait_recv()

            p, _ = item(i)

            @pl.when(p == core)
            def _():
                ring(i, True).start()

            @pl.when(p != core)
            def _():
                ring(i, False).start()

        keep.wait()

        @pl.when(core == 0)
        def _():
            to_up.wait_send()

        @pl.when(core == 1)
        def _():
            to_down.wait_send()

        @pl.loop(0, total)
        def _(i):
            ring(i, True).wait_send()

    @pl.when(z > 0)
    def _():
        base = row * rows_dev
        load.wait()

        pcol_s[...] = jnp.transpose(jnp.broadcast_to(piv[...], (128, width)))
        acc[...] = jnp.zeros_like(acc)

        @pl.loop(0, rows_dev // BLK)
        def _(b):
            lane = lax.broadcasted_iota(jnp.int32, (width, 128), 1) + (base + b * BLK)
            hit = [jnp.where(pcol_s[...] == lane + 128 * j, 1.0, 0.0).astype(BF16) for j in range(BLK // 128)]
            acc[...] += jnp.dot(jnp.concatenate(hit, axis=1), mv[pl.ds(pl.multiple_of(b * BLK, BLK), BLK), :],
                                preferred_element_type=F32)

        for h in range(2):
            pk[h] = acc[:, h * half:(h + 1) * half].astype(BF16)

        pl.semaphore_wait(bar, NX + NY - 1 + jnp.where(hop < NZ - 1, 1, 0))

        def send(src, dst, number, prow, recv=None):
            return pltpu.make_async_remote_copy(
                src, dst, bs.at[number], br.at[number if recv is None else recv],
                device_id={"prow": prow}, device_id_type=MESH)

        def xrow(k):
            return pl.ds(pl.multiple_of(k * xrows, xrows), xrows)

        def yrow(k):
            return pl.ds(pl.multiple_of(k * yrows, yrows), yrows)

        c_r1 = send(pk.at[1 - core], rc, R1, mate)
        c_r2 = [send(s1.at[xrow(xpeer(k))], rx.at[k - 1], R2 + k - 1, prow_of(xpeer(k), y)) for k in range(1, NX)]
        c_r3 = [send(s2.at[yrow(ypeer(k))], ry.at[k - 1], R3 + k - 1, prow_of(x, ypeer(k))) for k in range(1, NY)]
        c_g1 = [send(s3, g1.at[yrow(y)], G1 + k - 1, prow_of(x, ypeer(k))) for k in range(1, NY)]
        c_g2 = [send(g1, g.at[core, xrow(x)], G2 + k - 1, prow_of(xpeer(k), y)) for k in range(1, NX)]
        c_g3 = send(g.at[core], g.at[core], G3, mate)
        c_d0a = send(mv.at[pl.ds(0, width), pl.ds(half, half)], dd, D0A, mate)
        c_d0b = [send(mv.at[pl.ds(k * xrows, xrows), pl.ds(0, half)], db, D0B + k - 1, prow_of(k, y), D0B) for k in range(1, NX)]
        c_d0b1 = [send(dd.at[pl.ds(k * xrows, xrows)], db, D0B + k - 1, prow_of(k, y), D0B) for k in range(1, NX)]
        c_d0c = [send(db.at[pl.ds(k * yrows, yrows)], d0, D0C + k - 1, prow_of(x, k), D0C) for k in range(1, NY)]
        c_d1 = [send(d0, d1.at[yrow(y)], D1 + k - 1, prow_of(x, ypeer(k))) for k in range(1, NY)]
        c_d2 = [send(d1, d.at[core, xrow(x)], D2 + k - 1, prow_of(xpeer(k), y)) for k in range(1, NX)]
        c_d3 = send(d.at[core], d.at[core], D3, mate)
        l_dba = pltpu.make_async_copy(mv.at[pl.ds(0, xrows), pl.ds(0, half)], db, ls.at[1])
        l_dbb = pltpu.make_async_copy(dd.at[pl.ds(0, xrows)], db, ls.at[1])
        l_d0 = pltpu.make_async_copy(db.at[pl.ds(0, yrows)], d0, ls.at[4])
        l_d1 = pltpu.make_async_copy(d0, d1.at[yrow(y)], ls.at[1])
        l_d = pltpu.make_async_copy(d1, d.at[core, xrow(x)], ls.at[2])
        l_g = pltpu.make_async_copy(g1, g.at[core, xrow(x)], ls.at[3])
        first = (x == 0) & (y == 0)

        c_r1.start()

        @pl.when(first & (core == 0))
        def _():
            c_d0a.start()
            l_dba.start()
            for cp in c_d0b:
                cp.start()

        def step1():
            @pl.when(first & (core == 1))
            def _():
                c_d0a.wait_recv()
                l_dbb.start()
                for cp in c_d0b1:
                    cp.start()

        def step2():
            c_r1.wait_recv()
            s1[...] = (pk[core].astype(F32) + rc[...].astype(F32)).astype(BF16)
            for cp in c_r2:
                cp.start()

        def step3():
            @pl.when(y == 0)
            def _():
                @pl.when(x == 0)
                def _():
                    l_dba.wait()

                @pl.when(x > 0)
                def _():
                    c_d0b[0].wait_recv()

                l_d0.start()
                for cp in c_d0c:
                    cp.start()

        def step4():
            for cp in c_r2:
                cp.wait_recv()
            got = s1[xrow(x), :].astype(F32)
            for k in range(NX - 1):
                got += rx[k].astype(F32)
            s2[...] = got.astype(BF16)
            for cp in c_r3:
                cp.start()

        def step5():
            @pl.when(y == 0)
            def _():
                l_d0.wait()

            @pl.when(y > 0)
            def _():
                c_d0c[0].wait_recv()

            l_d1.start()
            for cp in c_d1:
                cp.start()

        def step6():
            for cp in c_r3:
                cp.wait_recv()
            got = s2[yrow(y), :].astype(F32)
            for k in range(NY - 1):
                got += ry[k].astype(F32)
            s3[...] = got.astype(BF16)
            g1[yrow(y), :] = got.astype(BF16)
            for cp in c_g1:
                cp.start()

        def step7():
            l_d1.wait()
            for cp in c_d1:
                cp.wait_recv()
            l_d.start()
            for cp in c_d2:
                cp.start()

        def step8():
            for cp in c_g1:
                cp.wait_recv()
            l_g.start()
            for cp in c_g2:
                cp.start()

        def step9():
            l_d.wait()
            for cp in c_d2:
                cp.wait_recv()
            c_d3.start()

        def step9b():
            c_d3.wait_recv()

        def step10():
            l_g.wait()
            for cp in c_g2:
                cp.wait_recv()
            c_g3.start()

        def step11():
            c_g3.wait_recv()
            for h in range(2):
                up[h] = jnp.dot(inv[...], g[h], preferred_element_type=F32).astype(BF16)

        def exchange(b):
            at = pl.ds(pl.multiple_of(b * BLK, BLK), BLK)
            hit = lax.broadcasted_iota(jnp.int32, (BLK, width), 0) + (base + b * BLK) == piv[...]
            one = jnp.where(hit, 1.0, 0.0)
            has = jnp.max(one, axis=1, keepdims=True) > 0.5
            one = one.astype(BF16)
            for h in range(2):
                here = slice(h * half, (h + 1) * half)
                moved = jnp.dot(one, d[h], preferred_element_type=F32)
                out[at, here] = jnp.where(has, moved, mv[at, here].astype(F32)).astype(BF16)

        def update(k):
            b = jnp.where(z < NZ // 2, k, rows_dev // BLK - 1 - k)
            at = pl.ds(pl.multiple_of(b * BLK, BLK), BLK)

            @pl.loop(0, BLK // R)
            def _(j):
                c = b * (BLK // R) + j

                @pl.when(jnp.logical_not(mine(c)))
                def _():
                    hand_over(c, core).wait_recv()

            lead = (row == 0) & (b < width // BLK)

            @pl.when(lead)
            def _():
                for h in range(2):
                    out[at, h * half:(h + 1) * half] = up[h, at, :]

            @pl.when(jnp.logical_not(lead))
            def _():
                left = pan[core, at, :]
                for h in range(2):
                    here = slice(h * half, (h + 1) * half)
                    out[at, here] = (out[at, here].astype(F32)
                                     - jnp.dot(left, up[h], preferred_element_type=F32)).astype(BF16)

        steps = ((24, step1), (25, step2), (41, step3), (44, step4), (58, step5), (65, step6), (77, step7), (85, step8),
                 (96, step9), (99, step9b), (104, step10), (110, step11))
        early = 3
        lag = jnp.where(core == 1, 5 + 5 * z, 4 + 9 * (NZ - z))

        @pl.loop(0, jnp.maximum(lag + n_in, 119))
        def _(t):
            for when, step in steps:
                pl.when(t == when)(step)

            @pl.when((t >= 99) & (t < 107))
            def _():
                exchange(t - 99)

            @pl.when((t >= 113) & (t < 113 + 2 * early) & (lax.rem(t, 2) == 1))
            def _():
                update((t - 113) // 2)

            i = t - lag

            @pl.when((i >= 0) & (i < n_in))
            def _():
                ring(i, False).wait_recv()

                @pl.when(i < n_out)
                def _():
                    ring(i, False).start()

                p, c = item(i)

                @pl.when(p != core)
                def _():
                    hand_over(c, p).start()

        @pl.loop(early, rows_dev // BLK)
        def _(k):
            update(k)

        @pl.loop(0, n_chunk)
        def _(c):
            @pl.when(mine(c))
            def _():
                hand_over(c, 1 - core).wait_send()

        @pl.loop(0, n_out)
        def _(i):
            ring(i, False).wait_send()

        for cp in [c_r1, *c_r2, *c_r3, *c_g1, *c_g2, c_g3, *c_d1, *c_d2, c_d3]:
            cp.wait_send()

        @pl.when(first & (core == 0))
        def _():
            c_d0a.wait_send()

        @pl.when(first)
        def _():
            for cp in c_d0b1:
                cp.wait_send()

        @pl.when(y == 0)
        def _():
            for cp in c_d0c:
                cp.wait_send()


def per_device(matrix, pivots, unit_inverse):
    rows, cols = matrix.shape
    width = unit_inverse.shape[0]
    half = cols // 2
    n_chunk = rows // R
    n_ring = 2 * N_BOTH + 2 * max(N_PLUS, n_chunk - N_PLUS - N_BOTH)
    xrows, yrows = width // NX, width // NX // NY
    dma = pltpu.SemaphoreType.DMA
    vm = pltpu.VMEM
    return pl.pallas_call(
        kernel,
        out_shape=pltpu.VMEM(matrix.shape, matrix.dtype),
        in_specs=[
            pl.BlockSpec(memory_space=pl.ANY),
            pl.BlockSpec(memory_space=pltpu.VMEM),
            pl.BlockSpec(memory_space=pltpu.VMEM),
        ],
        out_specs=pl.BlockSpec(memory_space=pltpu.VMEM),
        scratch_shapes=[
            vm((2, rows, cols), BF16),
            vm((rows, cols), BF16),
            vm((width, cols), F32),
            vm((width, 128), jnp.int32),
            vm((2, width, half), BF16),
            vm((width, half), BF16),
            vm((width, half), BF16),
            vm((NX - 1, xrows, half), BF16),
            vm((xrows, half), BF16),
            vm((NY - 1, yrows, half), BF16),
            vm((yrows, half), BF16),
            vm((xrows, half), BF16),
            vm((2, width, half), BF16),
            vm((width, half), BF16),
            vm((xrows, half), BF16),
            vm((yrows, half), BF16),
            vm((xrows, half), BF16),
            vm((2, width, half), BF16),
            vm((2, width, half), BF16),
            dma((n_ring,)),
            dma((n_ring,)),
            dma((n_chunk,)),
            dma((n_chunk,)),
            dma((NSEM,)),
            dma((NSEM,)),
            dma((5,)),
        ],
        compiler_params=pltpu.CompilerParams(collective_id=0, has_side_effects=True),
        name="lu_step",
    )(matrix, pivots.reshape(1, width), unit_inverse)


def solution(mesh):
    return jax.shard_map(
        per_device,
        mesh=mesh,
        in_specs=(P("prow", "pcol"), P(), P()),
        out_specs=P("prow", "pcol"),
        check_vma=False,
    )
```
